32 devices in a mesh: grp: 2 (over x), row: 16 (over z, y, core).
Axes of the slice: x: 2, y: 2, z: 4, core: 2. Of those that a mesh axis runs over, the one named last changes fastest.
Arguments:
- coordinates: float32 [3, 65536], P(None, ('grp', 'row')), parts along dimension 1, may hold values from -0.12 to 1.12, as said below
- length_scale: float32 [65536], P(('grp', 'row')), parts along dimension 0, may hold values from 0.05 to 0.4
- probes: bfloat16 [64, 65536], P(None, ('grp', 'row')), parts along dimension 1, may hold values from -6 to 6
- near_ids: int32 [256, 16], P(('grp', 'row')), parts along dimension 0, may hold values from 0 to 127, as said below
- near_count: int32 [256], P(('grp', 'row')), parts along dimension 0, may hold values from 8 to 16
- basis_out: bfloat16 [256, 32, 256], P(('grp', 'row')), parts along dimension 0, may hold values from -1 to 1
- basis_in: bfloat16 [256, 32, 256], P(('grp', 'row')), parts along dimension 0, may hold values from -0.375 to 0.375
Outputs:
- sampled: float32 [64, 65536], P(None, ('grp', 'row')), parts along dimension 1
The draws below stay inside these ranges and needn't reach their ends.
There are 2 independent parts, one for each index of `grp`. The reference program is written for one: setup_inputs(seed, part) draws one part's arguments, and reference() takes and returns one part's arrays. A program takes and returns all parts, laid end to end along the dimension named above; each array names one. Nothing has to cross between parts.
Inputs may be any that keep to these rules, and one draw needn't show every extreme that they name: `coordinates`: points of one block lie within 0.12 of a common center in every coordinate. `near_ids`: row i lists i itself first, then distinct blocks whose index differs from i by at most 8; the slots from near_count[i] on hold i again.
All inputs are finite; a program needn't handle non-finite values.
Results may differ from the reference program's by a relative error of at most 0.00055.
The reference program's roundings to bfloat16 on the way count: a program that leaves them out, or rounds other values in their place, can miss the bound.
Values may be sent and summed in bfloat16 or wider, within the bound.
A program may use at most 64 MiB of HBM per device.

```python
import math
import jax
import jax.numpy as jnp
from jax import lax

B = 256
P_SIZE = 64
R = 32
HALO = 8
NEARMAX = 16
NB = 128
N = 32768


def curve_centers(key):
    total_bits = max((NB - 1).bit_length(), 1)
    blocks = jnp.arange(NB).astype(jnp.int32)
    cells = [jnp.zeros((NB,), jnp.int32) for axis_id in range(3)]
    widths = [1, 1, 1]
    for bit in range(total_bits):
        axis_id = bit % 3
        digit = blocks // 2 ** bit % 2
        cells[axis_id] = cells[axis_id] + digit * widths[axis_id]
        widths[axis_id] = widths[axis_id] * 2
    jitter = jax.random.uniform(key, (NB, 3), jnp.float32, -0.25, 0.25)
    columns = []
    for axis_id in range(3):
        position = (cells[axis_id].astype(jnp.float32) + 0.5 + jitter[:, axis_id]) / float(widths[axis_id])
        columns.append(position)
    return jnp.stack(columns, axis=1)


def draw_coordinates(key, part):
    first_key, second_key = jax.random.split(jax.random.fold_in(key, 3))
    centers = curve_centers(first_key)
    spread = 0.06
    jitter = jax.random.uniform(second_key, (NB, B, 3), jnp.float32, -spread, spread)
    points = centers[:, None, :] + jitter
    return points.reshape(N, 3).T


def near_pattern(key):
    first_key, second_key = jax.random.split(jax.random.fold_in(key, 7))
    offsets = jnp.arange(-HALO, HALO + 1).astype(jnp.int32)
    window = 2 * HALO + 1
    blocks = jnp.arange(NB).astype(jnp.int32)[:, None]
    candidate = blocks + offsets[None, :]
    valid = (candidate >= 0) & (candidate < NB) & (offsets[None, :] != 0)
    scores = jax.random.randint(first_key, (NB, window), 0, 1 << 20) * (window + 1) + jnp.arange(window).astype(jnp.int32)[None, :]
    scores = jnp.where(offsets[None, :] == 0, -1, jnp.where(valid, scores, scores + (1 << 28)))
    order = jnp.argsort(scores, axis=1, stable=True)
    ranked = jnp.take_along_axis(candidate, order, axis=1)[:, :NEARMAX]
    usable = jnp.sum(valid.astype(jnp.int32), axis=1) + 1
    wanted = jax.random.randint(second_key, (NB,), HALO, NEARMAX + 1)
    wanted = jnp.where(jnp.arange(NB) == NB // 2, NEARMAX, wanted)
    counts = jnp.minimum(wanted, usable).astype(jnp.int32)
    listed = jnp.where(jnp.arange(NEARMAX)[None, :] < counts[:, None], ranked, blocks)
    return (listed.astype(jnp.int32), counts)


def draw_near_ids(key, part):
    return near_pattern(key)[0]


def draw_near_count(key, part):
    return near_pattern(key)[1]


def block_scale(own_key, extent, cuts, low, high):
    level = 1.0
    for dim, blocks in cuts:
        draws = jax.random.uniform(jax.random.fold_in(jax.random.fold_in(own_key, 6), dim), (blocks,), jnp.float32, low / len(cuts), high / len(cuts))
        level = level * jnp.repeat(jnp.exp(draws), extent[dim] // blocks).reshape((-1,) + (1,) * (len(extent) - 1 - dim))
    return level


def scatter_about(rng, shape, scale, limit, pieces=(), dtype=jnp.bfloat16):
    entries = scale * jax.random.normal(rng, shape, jnp.float32)
    if pieces:
        entries = entries * block_scale(rng, shape, pieces, -0.22, 0.18)
    return jnp.clip(entries, -limit, limit).astype(dtype)


def setup_inputs(seed: int = 0, part: int = 0) -> dict:
    key_of = jax.random.split(jax.random.key(seed), 8)
    part_keys = jax.random.split(jax.random.fold_in(key_of[7], part), 8)
    return {
        "coordinates": draw_coordinates(jax.random.fold_in(jax.random.fold_in(key_of[7], part), 71), part),
        "length_scale": jnp.clip(jnp.exp(math.log(0.4) - 2.0794415 * jax.random.uniform(part_keys[1], (N,), jnp.float32) ** block_scale(part_keys[1], (N,), ((0, 16),), -0.2, 0.2)), 0.05, 0.4),
        "probes": scatter_about(part_keys[2], (P_SIZE, N), 1.0, 6.0, ((1, 16),)),
        "near_ids": draw_near_ids(jax.random.fold_in(jax.random.fold_in(key_of[7], part), 71), part),
        "near_count": draw_near_count(jax.random.fold_in(jax.random.fold_in(key_of[7], part), 71), part),
        "basis_out": scatter_about(part_keys[5], (NB, R, B), R ** -0.5, 1.0, ((0, 16),)),
        "basis_in": scatter_about(part_keys[6], (NB, R, B), B ** -0.5, 0.375, ((0, 16),)),
    }


def matern(first, second):
    sq_dist = (first[0] - second[0]) * (first[0] - second[0])
    sq_dist = sq_dist + (first[1] - second[1]) * (first[1] - second[1])
    sq_dist = sq_dist + (first[2] - second[2]) * (first[2] - second[2])
    mean_sq = 0.5 * (first[3] * first[3] + second[3] * second[3])
    prefac = (first[3] * second[3] / mean_sq) ** 1.5
    scaled = jnp.sqrt(3.0) * jnp.sqrt(sq_dist / mean_sq)
    return prefac * (1.0 + scaled) * jnp.exp(-scaled)

def reference(coordinates, length_scale, probes, near_ids, near_count, basis_out, basis_in):
    records = jnp.concatenate([coordinates, length_scale[None, :]], axis=0)
    rec_blocks = records.reshape(4, NB, B)
    probe_blocks = probes.reshape(P_SIZE, NB, B)
    slots = jnp.arange(NEARMAX).astype(jnp.int32)

    def one_row(inputs):
        row_ids, row_count, index = inputs
        source = rec_blocks[:, row_ids]
        target = rec_blocks[:, index]
        tiles = matern(source[:, :, :, None], target[:, None, None, :])
        keep = (slots < row_count).astype(jnp.float32)
        tiles = (tiles * keep[:, None, None]).astype(jnp.bfloat16)
        source_probe = probe_blocks[:, row_ids]
        return jnp.einsum('psa,sab->pb', source_probe.astype(jnp.float32), tiles.astype(jnp.float32))
    near = lax.map(one_row, (near_ids, near_count, jnp.arange(NB).astype(jnp.int32)))
    near = jnp.transpose(near, (1, 0, 2))
    folded = jnp.einsum('jkb,pjb->jkp', basis_in.astype(jnp.float32), probe_blocks.astype(jnp.float32))
    folded = folded.astype(jnp.bfloat16).reshape(NB, R * P_SIZE)
    center = lax.optimization_barrier(jnp.mean(rec_blocks, axis=2))
    coupling = matern(center[:, :, None], center[:, None, :])
    every = jnp.arange(NB).astype(jnp.int32)
    is_near = jnp.any(near_ids[:, :, None] == every[None, None, :], axis=1)
    coupling = jnp.where(is_near, 0.0, coupling).astype(jnp.bfloat16)
    summed = jnp.dot(coupling, folded, preferred_element_type=jnp.float32).astype(jnp.bfloat16)
    summed = summed.reshape(NB, R, P_SIZE)
    far = jnp.einsum('ikp,ikb->pib', summed.astype(jnp.float32), basis_out.astype(jnp.float32))
    return (near + far).reshape(P_SIZE, N)
```

```python
import functools
import math

import jax
import jax.numpy as jnp
from jax import lax
from jax.experimental import pallas as pl
from jax.experimental.pallas import tpu as pltpu
from jax.sharding import PartitionSpec as P

HALO = 8
ROWS = 16
LOG2E = 1.0 / math.log(2.0)
C_SCALE = math.log(2.0) ** (-2.0 / 3.0)
D_SCALE = 3.0 * LOG2E * LOG2E * C_SCALE
F32 = jnp.float32
BF16 = jnp.bfloat16


def split3(x):
    high = x.astype(BF16)
    rest = x - high.astype(F32)
    mid = rest.astype(BF16)
    low = (rest - mid.astype(F32)).astype(BF16)
    return high, mid, low


def left_stack(x):
    h, m, l = [part.astype(F32) for part in split3(x)]
    return jnp.concatenate([h, h, m, h, l, m, m, l], axis=0)


def right_stack(x):
    h, m, l = split3(x)
    return jnp.concatenate([h, m, h, l, h, m, l, m], axis=0)


def matern(first, second):
    sq_dist = (first[0] - second[0]) * (first[0] - second[0])
    sq_dist = sq_dist + (first[1] - second[1]) * (first[1] - second[1])
    sq_dist = sq_dist + (first[2] - second[2]) * (first[2] - second[2])
    mean_sq = 0.5 * (first[3] * first[3] + second[3] * second[3])
    ratio = first[3] * second[3] / mean_sq
    prefac = ratio * jnp.sqrt(ratio)
    scaled = jnp.sqrt(3.0 * (sq_dist / mean_sq))
    return prefac * (1.0 + scaled) * jnp.exp(-scaled)


def nt(a, b):
    return lax.dot_general(a, b, (((1,), (1,)), ((), ())), preferred_element_type=F32)


def tn(a, b):
    return lax.dot_general(a, b, (((0,), (0,)), ((), ())), preferred_element_type=F32)


def nn(a, b):
    return lax.dot_general(a, b, (((1,), (0,)), ((), ())), preferred_element_type=F32)


def kernel(
    n, ob, bs,
    xyz_ref, len_ref, probes_ref, ids_ref, bout_ref, bin_ref, out_ref,
    xyz_r, len_r, probes_r, ids_r,
    rec_i, rec_j, cen_i, cen_j, lhs, rhs_c, mask_a, mask_b, acc, part,
    fold_all, cen_all,
    halo_send, halo_recv, part_send, part_recv, gat_send, gat_recv, cen_send, cen_recv,
):
    me = lax.axis_index("row")
    left = lax.rem(me + n - 1, n)
    right = lax.rem(me + 1, n)
    half = bin_ref.shape[1] // 2
    np_ = probes_ref.shape[0]
    width = n * ob

    barrier = pltpu.get_barrier_semaphore()

    def greet(k, carry):
        pl.semaphore_signal(barrier, inc=1, device_id={"row": lax.rem(me + k, n)})
        return carry

    lax.fori_loop(1, n, greet, 0)
    pl.semaphore_wait(barrier, n - 1)

    halo = [
        pltpu.make_async_remote_copy(
            src_ref=src, dst_ref=dst, send_sem=halo_send.at[k], recv_sem=halo_recv.at[k], device_id={"row": left}
        )
        for k, (src, dst) in enumerate(
            ((xyz_ref, xyz_r), (len_ref, len_r), (ids_ref, ids_r), (probes_ref, probes_r))
        )
    ]
    for copy in halo:
        copy.start()

    row = lax.broadcasted_iota(jnp.int32, (ROWS, bs), 0)

    def fill_j(xyz, length, base):
        rec_j[0:3, base : base + ob * bs] = xyz[...]
        rec_j[3:6, base : base + ob * bs] = jnp.ones((3, ob * bs), F32)
        rec_j[6:9, base : base + ob * bs] = xyz[...]
        rec_j[9:10, base : base + ob * bs] = jnp.ones((1, ob * bs), F32)
        ln = length[...]
        rec_j[10:11, base : base + ob * bs] = ln * ln
        rec_j[11:12, base : base + ob * bs] = 1.0 / ln
        rec_j[12:16, base : base + ob * bs] = jnp.zeros((4, ob * bs), F32)
        for b in range(ob):
            at = base + b * bs
            blk = rec_j[:, at : at + bs]
            inv = rec_j[11:12, at : at + bs]
            feat = jnp.where((row == 9) | (row == 10), blk, 0.0) * (inv * (0.5 * C_SCALE))
            rhs_c[base // bs + b] = right_stack(feat)

    rec_i[0:3, :] = xyz_ref[...]
    rec_i[3:6, :] = xyz_ref[...]
    rec_i[6:9, :] = jnp.ones((3, ob * bs), F32)
    ln0 = len_ref[...]
    rec_i[9:10, :] = ln0 * ln0
    rec_i[10:11, :] = jnp.ones((1, ob * bs), F32)
    rec_i[11:12, :] = ln0
    rec_i[12:16, :] = jnp.zeros((4, ob * bs), F32)
    fill_j(xyz_ref, len_ref, 0)

    lane = lax.broadcasted_iota(jnp.int32, (ROWS, 128), 1)
    own_centers = jnp.zeros((ROWS, 128), F32)
    for b in range(ob):
        blk = rec_i[:, b * bs : (b + 1) * bs]
        mean = jnp.sum(blk, axis=1, keepdims=True) * (1.0 / bs)
        own_centers = jnp.where(lane == b, mean, own_centers)
        mean_w = jnp.broadcast_to(mean, (ROWS, bs))
        cen = jnp.where(row < 6, mean_w, 0.0)
        v = blk - cen
        feat = jnp.where((row >= 3) & (row < 6), v * v, jnp.where(row < 11, v, 0.0)) * (1.0 / rec_i[11:12, b * bs : (b + 1) * bs])
        lhs[b] = left_stack(feat).T.astype(BF16)
        mean_j = jnp.sum(rec_j[:, b * bs : (b + 1) * bs], axis=1, keepdims=True) * (1.0 / bs)
        cen_j[b] = jnp.where((row < 3) | ((row >= 6) & (row < 9)), jnp.broadcast_to(mean_j, (ROWS, bs)), 0.0)
        pb = probes_ref[:, b * bs : (b + 1) * bs]
        fold = jnp.concatenate([nt(bin_ref[b, 0:half, :], pb), nt(bin_ref[b, half:, :], pb)], axis=1)
        fold_all[me, b * half : (b + 1) * half, :] = fold.astype(BF16)
    square = jnp.concatenate([own_centers, jnp.zeros((128 - ROWS, 128), F32)], axis=0).T
    own_cols = square[0:ob, :]
    cen_all[me] = own_cols

    def gather_copies(k):
        peer = lax.rem(me + k, n)
        return (
            pltpu.make_async_remote_copy(
                src_ref=fold_all.at[me], dst_ref=fold_all.at[me],
                send_sem=gat_send.at[k], recv_sem=gat_recv.at[k], device_id={"row": peer},
            ),
            pltpu.make_async_remote_copy(
                src_ref=cen_all.at[me], dst_ref=cen_all.at[me],
                send_sem=cen_send.at[k], recv_sem=cen_recv.at[k], device_id={"row": peer},
            ),
        )

    def gather_start(k, carry):
        for copy in gather_copies(k):
            copy.start()
        return carry

    lax.fori_loop(1, n, gather_start, 0)

    acc[...] = jnp.zeros_like(acc)

    def member(ids, target):
        return jnp.max(jnp.where(ids == target, 1.0, 0.0), axis=1, keepdims=True)

    def store_rows(ref, base, value):
        wide = jnp.broadcast_to(value, (ob, bs))
        for b in range(ob):
            ref[base + b] = wide[b : b + 1, :]

    ids = ids_ref[...]
    gid = lax.broadcasted_iota(jnp.int32, ids.shape, 0) + me * ob
    for dj in range(HALO + 1):
        store_rows(mask_a, dj * ob, member(ids, gid + dj))
        if dj:
            store_rows(mask_b, dj * 2 * ob, member(ids, gid - dj))
        else:
            store_rows(mask_b, 0, jnp.zeros((ob, 1), F32))

    def tile(i, jw, p_ref, p_base):
        dj = jw - i
        at = pl.multiple_of(jw * bs, bs)
        blk = rec_j[:, pl.ds(at, bs)]
        inv = rec_j[11:12, pl.ds(at, bs)]
        v = blk - cen_j[i]
        feat = jnp.where(
            row < 3, (-2.0 * D_SCALE) * v,
            jnp.where(row < 6, D_SCALE, jnp.where(row < 9, D_SCALE * v * v, 0.0)),
        ) * inv
        both = nn(lhs[i], jnp.concatenate([right_stack(feat), rhs_c[jw]], axis=1))
        dist = both[:, :bs]
        w = lax.rsqrt(both[:, bs:])
        w2 = w * w
        u = jnp.maximum(dist * w2, 1e-30)
        s = u * lax.rsqrt(u)
        value = ((w2 * w) * (LOG2E + s)) * jnp.exp2(-s)
        value = value.astype(BF16)
        p_j = p_ref[:, pl.ds(pl.multiple_of(p_base * bs, bs), bs)]
        p_i = probes_ref[:, pl.ds(pl.multiple_of(i * bs, bs), bs)]
        return (
            mask_a[dj * ob + i] * nt(p_j, value),
            mask_b[dj * 2 * ob + jw] * nn(p_i, value),
        )

    def triangle(g, s):
        c = (s + g) // ob
        a = g + c * (ob - 1 - 2 * g)
        return a, a + s - c * (ob - g)

    def own_group(g, carry):
        def step(s, inner):
            i, j = triangle(g, s)
            first, second = tile(i, j, probes_ref, j)
            acc[i] += first
            acc[j] += second
            return inner

        return lax.fori_loop(0, ob + 1, step, carry)

    lax.fori_loop(0, ob // 4, own_group, 0)

    for copy in halo:
        copy.wait()
    fill_j(xyz_r, len_r, ob * bs)
    ids2 = ids_r[...]
    for dj in range(1, HALO + 1):
        store_rows(mask_b, dj * 2 * ob + ob, member(ids2, gid + ob - dj))

    def part_copy(col):
        return pltpu.make_async_remote_copy(
            src_ref=acc.at[ob + col], dst_ref=part.at[col],
            send_sem=part_send.at[col], recv_sem=part_recv.at[col], device_id={"row": right},
        )

    def cross_group(g, carry):
        def step(s, inner):
            col, i = triangle(g, s)
            first, second = tile(i, ob + col, probes_r, col)
            acc[i] += first
            acc[ob + col] += second
            return inner

        lax.fori_loop(0, ob + 1, step, 0)
        part_copy(g).start()
        part_copy(ob - 1 - g).start()
        return carry

    lax.fori_loop(0, ob // 2, cross_group, 0)
    lax.fori_loop(ob // 4, ob // 2, own_group, 0)

    def gather_wait(k, carry):
        for copy in gather_copies(k):
            copy.wait()
        return carry

    lax.fori_loop(1, n, gather_wait, 0)
    centers = cen_all[...].reshape(width, 128).T
    picks = (0, 1, 2, 11)
    coupling = matern([own_cols[:, c : c + 1] for c in picks], [centers[c : c + 1, :] for c in picks])
    global_ids = lax.broadcasted_iota(jnp.int32, (ob, width), 1)
    near = jnp.zeros((ob, width), F32)
    for t in range(ids.shape[1]):
        near = jnp.where(ids[:, t : t + 1] == global_ids, 1.0, near)
    coupling = jnp.where(near > 0.0, 0.0, coupling).astype(BF16)

    step_w = 128
    total = jnp.zeros((ob * half, 2 * np_), F32)
    pick_r = lax.broadcasted_iota(jnp.int32, (step_w, step_w * half), 0)
    pick_c = lax.broadcasted_iota(jnp.int32, (step_w, step_w * half), 1)
    spread = jnp.where(pick_c // half == pick_r, 1.0, 0.0).astype(BF16)
    eye_r = lax.broadcasted_iota(jnp.int32, (ob * half, step_w * half), 0)
    eye_c = lax.broadcasted_iota(jnp.int32, (ob * half, step_w * half), 1)
    same = lax.rem(eye_r, half) == lax.rem(eye_c, half)
    per = step_w // ob
    for q in range(width // step_w):
        wide = nn(coupling[:, q * step_w : (q + 1) * step_w], spread)
        wide = jnp.concatenate(
            [jnp.broadcast_to(wide[i : i + 1, :], (half, step_w * half)) for i in range(ob)], axis=0
        )
        kron = jnp.where(same, wide, 0.0).astype(BF16)
        folded = fold_all[q * per : (q + 1) * per].reshape(step_w * half, 2 * np_)
        total = total + nn(kron, folded)
    summed = total.astype(BF16)

    for b in range(ob):
        part_copy(b).wait()
    for b in range(ob):
        mine = summed[b * half : (b + 1) * half, :]
        far = tn(mine[:, :np_], bout_ref[b, 0:half, :]) + tn(mine[:, np_:], bout_ref[b, half:, :])
        out_ref[:, b * bs : (b + 1) * bs] = acc[b] + part[b] + far


def solution(mesh):
    n = mesh.shape["row"]

    def shards(coordinates, length_scale, probes, near_ids, near_count, basis_out, basis_in):
        ob, rank, bs = basis_out.shape
        np_ = probes.shape[0]
        own = ob * bs
        slots = near_ids.shape[1]
        vmem = pl.BlockSpec(memory_space=pltpu.VMEM)
        dma = pltpu.SemaphoreType.DMA
        return pl.pallas_call(
            functools.partial(kernel, n, ob, bs),
            out_shape=jax.ShapeDtypeStruct((np_, own), F32),
            in_specs=[vmem] * 6,
            out_specs=vmem,
            scratch_shapes=[
                pltpu.VMEM((3, own), F32),
                pltpu.VMEM((1, own), F32),
                pltpu.VMEM((np_, own), BF16),
                pltpu.VMEM((ob, slots), jnp.int32),
                pltpu.VMEM((ROWS, own), F32),
                pltpu.VMEM((ROWS, 2 * own), F32),
                pltpu.VMEM((ob, ROWS, bs), F32),
                pltpu.VMEM((ob, ROWS, bs), F32),
                pltpu.VMEM((ob, bs, 8 * ROWS), BF16),
                pltpu.VMEM((2 * ob, 8 * ROWS, bs), BF16),
                pltpu.VMEM(((HALO + 1) * ob, 1, bs), F32),
                pltpu.VMEM(((HALO + 1) * 2 * ob, 1, bs), F32),
                pltpu.VMEM((2 * ob, np_, bs), F32),
                pltpu.VMEM((ob, np_, bs), F32),
                pltpu.VMEM((n, ob * rank // 2, 2 * np_), BF16),
                pltpu.VMEM((n, ob, 128), F32),
                dma((4,)), dma((4,)), dma((ob,)), dma((ob,)),
                dma((n,)), dma((n,)), dma((n,)), dma((n,)),
            ],
            compiler_params=pltpu.CompilerParams(collective_id=0, has_side_effects=True, vmem_limit_bytes=48 * 1024 * 1024),
        )(coordinates, length_scale.reshape(1, own), probes, near_ids, basis_out, basis_in)

    placed = (
        P(None, ("grp", "row")),
        P(("grp", "row")),
        P(None, ("grp", "row")),
        P(("grp", "row"), None),
        P(("grp", "row")),
        P(("grp", "row"), None, None),
        P(("grp", "row"), None, None),
    )
    return jax.shard_map(
        shards, mesh=mesh, in_specs=placed, out_specs=P(None, ("grp", "row")), check_vma=False
    )
```

```python
import functools
import math

import jax
import jax.numpy as jnp
from jax import lax
from jax.experimental import pallas as pl
from jax.experimental.pallas import tpu as pltpu
from jax.sharding import PartitionSpec as P

HALO = 8
ROWS = 16
CHUNKS = 1
LOG2E = 1.0 / math.log(2.0)
C_SCALE = math.log(2.0) ** (-2.0 / 3.0)
D_SCALE = 3.0 * LOG2E * LOG2E * C_SCALE
F32 = jnp.float32
BF16 = jnp.bfloat16


def split3(x):
    high = x.astype(BF16)
    rest = x - high.astype(F32)
    mid = rest.astype(BF16)
    low = (rest - mid.astype(F32)).astype(BF16)
    return high, mid, low


def left_stack(x):
    h, m, l = [part.astype(F32) for part in split3(x)]
    return jnp.concatenate([h, h, m, h, l, m, m, l], axis=0)


def right_stack(x):
    h, m, l = split3(x)
    return jnp.concatenate([h, m, h, l, h, m, l, m], axis=0)


def matern(first, second):
    sq_dist = (first[0] - second[0]) * (first[0] - second[0])
    sq_dist = sq_dist + (first[1] - second[1]) * (first[1] - second[1])
    sq_dist = sq_dist + (first[2] - second[2]) * (first[2] - second[2])
    mean_sq = 0.5 * (first[3] * first[3] + second[3] * second[3])
    ratio = first[3] * second[3] / mean_sq
    prefac = ratio * jnp.sqrt(ratio)
    scaled = jnp.sqrt(3.0 * (sq_dist / mean_sq))
    return prefac * (1.0 + scaled) * jnp.exp(-scaled)


def nt(a, b):
    return lax.dot_general(a, b, (((1,), (1,)), ((), ())), preferred_element_type=F32)


def tn(a, b):
    return lax.dot_general(a, b, (((0,), (0,)), ((), ())), preferred_element_type=F32)


def nn(a, b):
    return lax.dot_general(a, b, (((1,), (0,)), ((), ())), preferred_element_type=F32)


def kernel(
    n, ob, bs,
    xyz_in, len_in, probes_in, ids_in, bout_in, bin_in, out_ref,
    xyz_ref, len_ref, probes_ref, ids_ref, bout_ref, bin_ref,
    xyz_r, len_r, probes_r, ids_r,
    rec_i, rec_j, cen_i, cen_j, lhs, rhs_c, mask_a, mask_b, acc, part,
    fold_all, cen_all,
    value_buf, load_sem, halo_send, halo_recv, part_send, part_recv, gat_send, gat_recv, cen_send, cen_recv,
):
    me = lax.axis_index("row")
    left = lax.rem(me + n - 1, n)
    right = lax.rem(me + 1, n)
    half = bin_ref.shape[1] // 2
    loads = [
        pltpu.make_async_copy(src, dst, load_sem.at[k])
        for k, (src, dst) in enumerate(
            (
                (xyz_in, xyz_ref), (len_in, len_ref), (ids_in, ids_ref),
                (probes_in, probes_ref), (bin_in, bin_ref), (bout_in, bout_ref),
            )
        )
    ]
    for load in loads:
        load.start()
    np_ = probes_ref.shape[0]
    width = n * ob

    barrier = pltpu.get_barrier_semaphore()

    def greet(k, carry):
        pl.semaphore_signal(barrier, inc=1, device_id={"row": lax.rem(me + k, n)})
        return carry

    lax.fori_loop(1, n, greet, 0)
    pl.semaphore_wait(barrier, n - 1)

    halo = [
        pltpu.make_async_remote_copy(
            src_ref=src, dst_ref=dst, send_sem=halo_send.at[k], recv_sem=halo_recv.at[k], device_id={"row": left}
        )
        for k, (src, dst) in enumerate(
            ((xyz_in, xyz_r), (len_in, len_r), (ids_in, ids_r), (probes_in, probes_r))
        )
    ]
    for copy in halo:
        copy.start()

    for load in loads[:5]:
        load.wait()
    row = lax.broadcasted_iota(jnp.int32, (ROWS, bs), 0)

    def fill_j(xyz, length, base):
        rec_j[0:3, base : base + ob * bs] = xyz[...]
        rec_j[3:6, base : base + ob * bs] = jnp.ones((3, ob * bs), F32)
        rec_j[6:9, base : base + ob * bs] = xyz[...]
        rec_j[9:10, base : base + ob * bs] = jnp.ones((1, ob * bs), F32)
        ln = length[...]
        rec_j[10:11, base : base + ob * bs] = ln * ln
        rec_j[11:12, base : base + ob * bs] = 1.0 / ln
        rec_j[12:16, base : base + ob * bs] = jnp.zeros((4, ob * bs), F32)
        for b in range(ob):
            at = base + b * bs
            blk = rec_j[:, at : at + bs]
            inv = rec_j[11:12, at : at + bs]
            feat = jnp.where((row == 9) | (row == 10), blk, 0.0) * (inv * (0.5 * C_SCALE))
            rhs_c[base // bs + b] = right_stack(feat)

    rec_i[0:3, :] = xyz_ref[...]
    rec_i[3:6, :] = xyz_ref[...]
    rec_i[6:9, :] = jnp.ones((3, ob * bs), F32)
    ln0 = len_ref[...]
    rec_i[9:10, :] = ln0 * ln0
    rec_i[10:11, :] = jnp.ones((1, ob * bs), F32)
    rec_i[11:12, :] = ln0
    rec_i[12:16, :] = jnp.zeros((4, ob * bs), F32)
    fill_j(xyz_ref, len_ref, 0)

    lane = lax.broadcasted_iota(jnp.int32, (ROWS, 128), 1)
    own_centers = jnp.zeros((ROWS, 128), F32)
    for b in range(ob):
        blk = rec_i[:, b * bs : (b + 1) * bs]
        mean = jnp.sum(blk, axis=1, keepdims=True) * (1.0 / bs)
        own_centers = jnp.where(lane == b, mean, own_centers)
        mean_w = jnp.broadcast_to(mean, (ROWS, bs))
        cen = jnp.where(row < 6, mean_w, 0.0)
        v = blk - cen
        feat = jnp.where((row >= 3) & (row < 6), v * v, jnp.where(row < 11, v, 0.0)) * (1.0 / rec_i[11:12, b * bs : (b + 1) * bs])
        lhs[b] = left_stack(feat).T.astype(BF16)
        mean_j = jnp.sum(rec_j[:, b * bs : (b + 1) * bs], axis=1, keepdims=True) * (1.0 / bs)
        cen_j[b] = jnp.where((row < 3) | ((row >= 6) & (row < 9)), jnp.broadcast_to(mean_j, (ROWS, bs)), 0.0)
        pb = probes_ref[:, b * bs : (b + 1) * bs]
        fold = jnp.concatenate([nt(bin_ref[b, 0:half, :], pb), nt(bin_ref[b, half:, :], pb)], axis=1)
        fold_all[me, b * half : (b + 1) * half, :] = fold.astype(BF16)
    square = jnp.concatenate([own_centers, jnp.zeros((128 - ROWS, 128), F32)], axis=0).T
    own_cols = square[0:ob, :]
    cen_all[me] = own_cols

    def gather_copies(k):
        peer = lax.rem(me + k, n)
        return (
            pltpu.make_async_remote_copy(
                src_ref=fold_all.at[me], dst_ref=fold_all.at[me],
                send_sem=gat_send.at[k], recv_sem=gat_recv.at[k], device_id={"row": peer},
            ),
            pltpu.make_async_remote_copy(
                src_ref=cen_all.at[me], dst_ref=cen_all.at[me],
                send_sem=cen_send.at[k], recv_sem=cen_recv.at[k], device_id={"row": peer},
            ),
        )

    def gather_start(k, carry):
        for copy in gather_copies(k):
            copy.start()
        return carry

    lax.fori_loop(1, n, gather_start, 0)

    acc[...] = jnp.zeros_like(acc)

    def member(ids, target):
        return jnp.max(jnp.where(ids == target, 1.0, 0.0), axis=1, keepdims=True)

    def store_rows(ref, base, value):
        wide = jnp.broadcast_to(value, (ob, bs))
        for b in range(ob):
            ref[base + b] = wide[b : b + 1, :]

    ids = ids_ref[...]
    gid = lax.broadcasted_iota(jnp.int32, ids.shape, 0) + me * ob
    for dj in range(HALO + 1):
        store_rows(mask_a, dj * ob, member(ids, gid + dj))
        if dj:
            store_rows(mask_b, dj * 2 * ob, member(ids, gid - dj))
        else:
            store_rows(mask_b, 0, jnp.zeros((ob, 1), F32))

    rows = bs // CHUNKS

    def right_side(i, jw):
        at = pl.multiple_of(jw * bs, bs)
        v = rec_j[:, pl.ds(at, bs)] - cen_j[i]
        feat = jnp.where(
            row < 3, (-2.0 * D_SCALE) * v,
            jnp.where(row < 6, D_SCALE, jnp.where(row < 9, D_SCALE * v * v, 0.0)),
        ) * rec_j[11:12, pl.ds(at, bs)]
        return jnp.concatenate([right_stack(feat), rhs_c[jw]], axis=1)

    def entries(i, side, c):
        return nn(lhs[i, c * rows : (c + 1) * rows, :], side)

    def values(both):
        w = lax.rsqrt(both[:, bs:])
        w2 = w * w
        u = jnp.maximum(both[:, :bs] * w2, 1e-30)
        s = u * lax.rsqrt(u)
        return (((w2 * w) * (LOG2E + s)) * jnp.exp2(-s)).astype(BF16)

    def products(i, jw, p_ref, p_base, slot):
        dj = jw - i
        value = value_buf[slot]
        p_j = p_ref[:, pl.ds(pl.multiple_of(p_base * bs, bs), bs)]
        p_i = probes_ref[:, pl.ds(pl.multiple_of(i * bs, bs), bs)]
        acc[i] += mask_a[dj * ob + i] * nt(p_j, value)
        acc[jw] += mask_b[dj * 2 * ob + jw] * nn(p_i, value)

    def sweep(pairs, p_ref):
        side = right_side(pairs[0][0], pairs[0][1])
        current = [entries(pairs[0][0], side, c) for c in range(CHUNKS)]
        for t, (i, jw, p_base) in enumerate(pairs):
            upcoming = None
            if t + 1 < len(pairs):
                upcoming = right_side(pairs[t + 1][0], pairs[t + 1][1])
            following = []
            for c in range(CHUNKS):
                if upcoming is not None:
                    following.append(entries(pairs[t + 1][0], upcoming, c))
                value_buf[t % 2, c * rows : (c + 1) * rows, :] = values(current[c])
                if c == 0 and t:
                    products(*pairs[t - 1][:2], p_ref, pairs[t - 1][2], (t - 1) % 2)
            current = following
        last = len(pairs) - 1
        products(*pairs[last][:2], p_ref, pairs[last][2], last % 2)

    def triangle(g, s):
        c = (s + g) // ob
        a = g + c * (ob - 1 - 2 * g)
        return a, a + s - c * (ob - g)

    def own_group(g, carry):
        pairs = []
        for s in range(ob + 1):
            i, j = triangle(g, s)
            pairs.append((i, j, j))
        sweep(pairs, probes_ref)
        return carry

    lax.fori_loop(0, ob // 4, own_group, 0)

    for copy in halo:
        copy.wait()
    fill_j(xyz_r, len_r, ob * bs)
    ids2 = ids_r[...]
    for dj in range(1, HALO + 1):
        store_rows(mask_b, dj * 2 * ob + ob, member(ids2, gid + ob - dj))

    def part_copy(col):
        return pltpu.make_async_remote_copy(
            src_ref=acc.at[ob + col], dst_ref=part.at[col],
            send_sem=part_send.at[col], recv_sem=part_recv.at[col], device_id={"row": right},
        )

    def cross_group(g, carry):
        pairs = []
        for s in range(ob + 1):
            col, i = triangle(g, s)
            pairs.append((i, ob + col, col))
        sweep(pairs, probes_r)
        part_copy(g).start()
        part_copy(ob - 1 - g).start()
        return carry

    lax.fori_loop(0, ob // 2, cross_group, 0)
    lax.fori_loop(ob // 4, ob // 2, own_group, 0)

    def gather_wait(k, carry):
        for copy in gather_copies(k):
            copy.wait()
        return carry

    lax.fori_loop(1, n, gather_wait, 0)
    centers = cen_all[...].reshape(width, 128).T
    picks = (0, 1, 2, 11)
    coupling = matern([own_cols[:, c : c + 1] for c in picks], [centers[c : c + 1, :] for c in picks])
    global_ids = lax.broadcasted_iota(jnp.int32, (ob, width), 1)
    near = jnp.zeros((ob, width), F32)
    for t in range(ids.shape[1]):
        near = jnp.where(ids[:, t : t + 1] == global_ids, 1.0, near)
    coupling = jnp.where(near > 0.0, 0.0, coupling).astype(BF16)

    step_w = 128
    total = jnp.zeros((ob * half, 2 * np_), F32)
    pick_r = lax.broadcasted_iota(jnp.int32, (step_w, step_w * half), 0)
    pick_c = lax.broadcasted_iota(jnp.int32, (step_w, step_w * half), 1)
    spread = jnp.where(pick_c // half == pick_r, 1.0, 0.0).astype(BF16)
    eye_r = lax.broadcasted_iota(jnp.int32, (ob * half, step_w * half), 0)
    eye_c = lax.broadcasted_iota(jnp.int32, (ob * half, step_w * half), 1)
    same = lax.rem(eye_r, half) == lax.rem(eye_c, half)
    per = step_w // ob
    for q in range(width // step_w):
        wide = nn(coupling[:, q * step_w : (q + 1) * step_w], spread)
        wide = jnp.concatenate(
            [jnp.broadcast_to(wide[i : i + 1, :], (half, step_w * half)) for i in range(ob)], axis=0
        )
        kron = jnp.where(same, wide, 0.0).astype(BF16)
        folded = fold_all[q * per : (q + 1) * per].reshape(step_w * half, 2 * np_)
        total = total + nn(kron, folded)
    summed = total.astype(BF16)

    loads[5].wait()
    for b in range(ob):
        part_copy(b).wait()
    for b in range(ob):
        mine = summed[b * half : (b + 1) * half, :]
        far = tn(mine[:, :np_], bout_ref[b, 0:half, :]) + tn(mine[:, np_:], bout_ref[b, half:, :])
        out_ref[:, b * bs : (b + 1) * bs] = acc[b] + part[b] + far


def solution(mesh):
    n = mesh.shape["row"]

    def shards(coordinates, length_scale, probes, near_ids, near_count, basis_out, basis_in):
        ob, rank, bs = basis_out.shape
        np_ = probes.shape[0]
        own = ob * bs
        slots = near_ids.shape[1]
        vmem = pl.BlockSpec(memory_space=pltpu.VMEM)
        dma = pltpu.SemaphoreType.DMA
        return pl.pallas_call(
            functools.partial(kernel, n, ob, bs),
            out_shape=jax.ShapeDtypeStruct((np_, own), F32),
            in_specs=[pl.BlockSpec(memory_space=pl.ANY)] * 6,
            out_specs=vmem,
            scratch_shapes=[
                pltpu.VMEM((3, own), F32),
                pltpu.VMEM((1, own), F32),
                pltpu.VMEM((np_, own), BF16),
                pltpu.VMEM((ob, slots), jnp.int32),
                pltpu.VMEM((ob, rank, bs), BF16),
                pltpu.VMEM((ob, rank, bs), BF16),
                pltpu.VMEM((3, own), F32),
                pltpu.VMEM((1, own), F32),
                pltpu.VMEM((np_, own), BF16),
                pltpu.VMEM((ob, slots), jnp.int32),
                pltpu.VMEM((ROWS, own), F32),
                pltpu.VMEM((ROWS, 2 * own), F32),
                pltpu.VMEM((ob, ROWS, bs), F32),
                pltpu.VMEM((ob, ROWS, bs), F32),
                pltpu.VMEM((ob, bs, 8 * ROWS), BF16),
                pltpu.VMEM((2 * ob, 8 * ROWS, bs), BF16),
                pltpu.VMEM(((HALO + 1) * ob, 1, bs), F32),
                pltpu.VMEM(((HALO + 1) * 2 * ob, 1, bs), F32),
                pltpu.VMEM((2 * ob, np_, bs), F32),
                pltpu.VMEM((ob, np_, bs), F32),
                pltpu.VMEM((n, ob * rank // 2, 2 * np_), BF16),
                pltpu.VMEM((n, ob, 128), F32),
                pltpu.VMEM((2, bs, bs), BF16),
                dma((6,)), dma((4,)), dma((4,)), dma((ob,)), dma((ob,)),
                dma((n,)), dma((n,)), dma((n,)), dma((n,)),
            ],
            compiler_params=pltpu.CompilerParams(collective_id=0, has_side_effects=True, vmem_limit_bytes=60 * 1024 * 1024),
        )(coordinates, length_scale.reshape(1, own), probes, near_ids, basis_out, basis_in)

    placed = (
        P(None, ("grp", "row")),
        P(("grp", "row")),
        P(None, ("grp", "row")),
        P(("grp", "row"), None),
        P(("grp", "row")),
        P(("grp", "row"), None, None),
        P(("grp", "row"), None, None),
    )
    return jax.shard_map(
        shards, mesh=mesh, in_specs=placed, out_specs=P(None, ("grp", "row")), check_vma=False
    )
```

```python
import functools
import math

import jax
import jax.numpy as jnp
from jax import lax
from jax.experimental import pallas as pl
from jax.experimental.pallas import tpu as pltpu
from jax.sharding import PartitionSpec as P

HALO = 8
ROWS = 16
CHUNKS = 1
LOG2E = 1.0 / math.log(2.0)
C_SCALE = math.log(2.0) ** (-2.0 / 3.0)
D_SCALE = 3.0 * LOG2E * LOG2E * C_SCALE
F32 = jnp.float32
BF16 = jnp.bfloat16


def split3(x):
    high = x.astype(BF16)
    rest = x - high.astype(F32)
    mid = rest.astype(BF16)
    low = (rest - mid.astype(F32)).astype(BF16)
    return high, mid, low


def left_stack(x):
    h, m, l = [part.astype(F32) for part in split3(x)]
    return jnp.concatenate([h, h, m, h, l, m, m, l], axis=0)


def right_stack(x):
    h, m, l = split3(x)
    return jnp.concatenate([h, m, h, l, h, m, l, m], axis=0)


def matern(first, second):
    sq_dist = (first[0] - second[0]) * (first[0] - second[0])
    sq_dist = sq_dist + (first[1] - second[1]) * (first[1] - second[1])
    sq_dist = sq_dist + (first[2] - second[2]) * (first[2] - second[2])
    mean_sq = 0.5 * (first[3] * first[3] + second[3] * second[3])
    ratio = first[3] * second[3] / mean_sq
    prefac = ratio * jnp.sqrt(ratio)
    scaled = jnp.sqrt(3.0 * (sq_dist / mean_sq))
    return prefac * (1.0 + scaled) * jnp.exp(-scaled)


def nt(a, b):
    return lax.dot_general(a, b, (((1,), (1,)), ((), ())), preferred_element_type=F32)


def tn(a, b):
    return lax.dot_general(a, b, (((0,), (0,)), ((), ())), preferred_element_type=F32)


def nn(a, b):
    return lax.dot_general(a, b, (((1,), (0,)), ((), ())), preferred_element_type=F32)


def kernel(
    n, ob, bs,
    xyz_in, len_in, probes_in, ids_in, bout_in, bin_in, out_ref,
    xyz_ref, len_ref, probes_ref, ids_ref, bout_ref, bin_ref,
    xyz_r, len_r, probes_r, ids_r,
    rec_i, rec_j, cen_i, cen_j, lhs, rhs_c, mask_a, mask_b, acc, part,
    fold_all, cen_all,
    value_buf, load_sem, halo_send, halo_recv, part_send, part_recv, gat_send, gat_recv, cen_send, cen_recv,
):
    me = lax.axis_index("row")
    left = lax.rem(me + n - 1, n)
    right = lax.rem(me + 1, n)
    half = bin_ref.shape[1] // 2
    loads = [
        pltpu.make_async_copy(src, dst, load_sem.at[k])
        for k, (src, dst) in enumerate(
            (
                (xyz_in, xyz_ref), (len_in, len_ref), (ids_in, ids_ref),
                (probes_in, probes_ref), (bin_in, bin_ref), (bout_in, bout_ref),
            )
        )
    ]
    for load in loads:
        load.start()
    np_ = probes_ref.shape[0]
    width = n * ob

    barrier = pltpu.get_barrier_semaphore()

    def greet(k, carry):
        pl.semaphore_signal(barrier, inc=1, device_id={"row": lax.rem(me + k, n)})
        return carry

    lax.fori_loop(1, n, greet, 0)
    pl.semaphore_wait(barrier, n - 1)

    halo = [
        pltpu.make_async_remote_copy(
            src_ref=src, dst_ref=dst, send_sem=halo_send.at[k], recv_sem=halo_recv.at[k], device_id={"row": left}
        )
        for k, (src, dst) in enumerate(
            ((xyz_in, xyz_r), (len_in, len_r), (ids_in, ids_r), (probes_in, probes_r))
        )
    ]
    for copy in halo:
        copy.start()

    for load in loads[:5]:
        load.wait()
    row = lax.broadcasted_iota(jnp.int32, (ROWS, bs), 0)

    def fill_j(xyz, length, base):
        rec_j[0:3, base : base + ob * bs] = xyz[...]
        rec_j[3:6, base : base + ob * bs] = jnp.ones((3, ob * bs), F32)
        rec_j[6:9, base : base + ob * bs] = xyz[...]
        rec_j[9:10, base : base + ob * bs] = jnp.ones((1, ob * bs), F32)
        ln = length[...]
        rec_j[10:11, base : base + ob * bs] = ln * ln
        rec_j[11:12, base : base + ob * bs] = 1.0 / ln
        rec_j[12:16, base : base + ob * bs] = jnp.zeros((4, ob * bs), F32)
        for b in range(ob):
            at = base + b * bs
            blk = rec_j[:, at : at + bs]
            inv = rec_j[11:12, at : at + bs]
            feat = jnp.where((row == 9) | (row == 10), blk, 0.0) * (inv * (0.5 * C_SCALE))
            rhs_c[base // bs + b] = right_stack(feat)

    rec_i[0:3, :] = xyz_ref[...]
    rec_i[3:6, :] = xyz_ref[...]
    rec_i[6:9, :] = jnp.ones((3, ob * bs), F32)
    ln0 = len_ref[...]
    rec_i[9:10, :] = ln0 * ln0
    rec_i[10:11, :] = jnp.ones((1, ob * bs), F32)
    rec_i[11:12, :] = ln0
    rec_i[12:16, :] = jnp.zeros((4, ob * bs), F32)
    fill_j(xyz_ref, len_ref, 0)

    lane = lax.broadcasted_iota(jnp.int32, (ROWS, 128), 1)
    own_centers = jnp.zeros((ROWS, 128), F32)
    for b in range(ob):
        blk = rec_i[:, b * bs : (b + 1) * bs]
        mean = jnp.sum(blk, axis=1, keepdims=True) * (1.0 / bs)
        own_centers = jnp.where(lane == b, mean, own_centers)
        mean_w = jnp.broadcast_to(mean, (ROWS, bs))
        cen = jnp.where(row < 6, mean_w, 0.0)
        v = blk - cen
        feat = jnp.where((row >= 3) & (row < 6), v * v, jnp.where(row < 11, v, 0.0)) * (1.0 / rec_i[11:12, b * bs : (b + 1) * bs])
        lhs[b] = left_stack(feat).T.astype(BF16)
        mean_j = jnp.sum(rec_j[:, b * bs : (b + 1) * bs], axis=1, keepdims=True) * (1.0 / bs)
        cen_j[b] = jnp.where((row < 3) | ((row >= 6) & (row < 9)), jnp.broadcast_to(mean_j, (ROWS, bs)), 0.0)
        pb = probes_ref[:, b * bs : (b + 1) * bs]
        fold = jnp.concatenate([nt(bin_ref[b, 0:half, :], pb), nt(bin_ref[b, half:, :], pb)], axis=1)
        fold_all[me, b * half : (b + 1) * half, :] = fold.astype(BF16)
    square = jnp.concatenate([own_centers, jnp.zeros((128 - ROWS, 128), F32)], axis=0).T
    own_cols = square[0:ob, :]
    cen_all[me] = own_cols

    def gather_copies(k):
        peer = lax.rem(me + k, n)
        return (
            pltpu.make_async_remote_copy(
                src_ref=fold_all.at[me], dst_ref=fold_all.at[me],
                send_sem=gat_send.at[k], recv_sem=gat_recv.at[k], device_id={"row": peer},
            ),
            pltpu.make_async_remote_copy(
                src_ref=cen_all.at[me], dst_ref=cen_all.at[me],
                send_sem=cen_send.at[k], recv_sem=cen_recv.at[k], device_id={"row": peer},
            ),
        )

    def gather_start(k, carry):
        for copy in gather_copies(k):
            copy.start()
        return carry

    lax.fori_loop(1, n, gather_start, 0)

    acc[...] = jnp.zeros_like(acc)

    def member(ids, target):
        return jnp.max(jnp.where(ids == target, 1.0, 0.0), axis=1, keepdims=True)

    def store_rows(ref, base, value):
        wide = jnp.broadcast_to(value, (ob, bs))
        for b in range(ob):
            ref[base + b] = wide[b : b + 1, :]

    ids = ids_ref[...]
    gid = lax.broadcasted_iota(jnp.int32, ids.shape, 0) + me * ob
    for dj in range(HALO + 1):
        store_rows(mask_a, dj * ob, member(ids, gid + dj))
        if dj:
            store_rows(mask_b, dj * 2 * ob, member(ids, gid - dj))
        else:
            store_rows(mask_b, 0, jnp.zeros((ob, 1), F32))

    rows = bs // CHUNKS

    def right_side(i, jw):
        at = pl.multiple_of(jw * bs, bs)
        v = rec_j[:, pl.ds(at, bs)] - cen_j[i]
        feat = jnp.where(
            row < 3, (-2.0 * D_SCALE) * v,
            jnp.where(row < 6, D_SCALE, jnp.where(row < 9, D_SCALE * v * v, 0.0)),
        ) * rec_j[11:12, pl.ds(at, bs)]
        return jnp.concatenate([right_stack(feat), rhs_c[jw]], axis=1)

    def entries(i, side, c):
        return nn(lhs[i, c * rows : (c + 1) * rows, :], side)

    def values(both):
        w = lax.rsqrt(both[:, bs:])
        w2 = w * w
        u = jnp.maximum(both[:, :bs] * w2, 1e-30)
        s = u * lax.rsqrt(u)
        return (((w2 * w) * (LOG2E + s)) * jnp.exp2(-s)).astype(BF16)

    def products(i, jw, p_ref, p_base, slot):
        dj = jw - i
        value = value_buf[slot]
        p_j = p_ref[:, pl.ds(pl.multiple_of(p_base * bs, bs), bs)]
        p_i = probes_ref[:, pl.ds(pl.multiple_of(i * bs, bs), bs)]
        acc[i] += mask_a[dj * ob + i] * nt(p_j, value)
        acc[jw] += mask_b[dj * 2 * ob + jw] * nn(p_i, value)

    def sweep(pairs, p_ref):
        side = right_side(pairs[0][0], pairs[0][1])
        current = [entries(pairs[0][0], side, c) for c in range(CHUNKS)]
        for t, (i, jw, p_base) in enumerate(pairs):
            upcoming = None
            if t + 1 < len(pairs):
                upcoming = right_side(pairs[t + 1][0], pairs[t + 1][1])
            following = []
            for c in range(CHUNKS):
                if upcoming is not None:
                    following.append(entries(pairs[t + 1][0], upcoming, c))
                value_buf[t % 2, c * rows : (c + 1) * rows, :] = values(current[c])
                if c == 0 and t:
                    products(*pairs[t - 1][:2], p_ref, pairs[t - 1][2], (t - 1) % 2)
            current = following
        last = len(pairs) - 1
        products(*pairs[last][:2], p_ref, pairs[last][2], last % 2)

    def triangle(g, s):
        c = (s + g) // ob
        a = g + c * (ob - 1 - 2 * g)
        return a, a + s - c * (ob - g)

    def own_groups(first, last):
        pairs = []
        for g in range(first, last):
            for s in range(ob + 1):
                i, j = triangle(g, s)
                pairs.append((i, j, j))
        sweep(pairs, probes_ref)

    own_groups(0, ob // 4)

    for copy in halo:
        copy.wait()
    fill_j(xyz_r, len_r, ob * bs)
    ids2 = ids_r[...]
    for dj in range(1, HALO + 1):
        store_rows(mask_b, dj * 2 * ob + ob, member(ids2, gid + ob - dj))

    def part_copy(col):
        return pltpu.make_async_remote_copy(
            src_ref=acc.at[ob + col], dst_ref=part.at[col],
            send_sem=part_send.at[col], recv_sem=part_recv.at[col], device_id={"row": right},
        )

    def cross_groups(h, carry):
        pairs = []
        for g in (2 * h, 2 * h + 1):
            for s in range(ob + 1):
                col, i = triangle(g, s)
                pairs.append((i, ob + col, col))
        sweep(pairs, probes_r)
        for g in (2 * h, 2 * h + 1):
            part_copy(g).start()
            part_copy(ob - 1 - g).start()
        return carry

    lax.fori_loop(0, ob // 4, cross_groups, 0)
    own_groups(ob // 4, ob // 2)

    def gather_wait(k, carry):
        for copy in gather_copies(k):
            copy.wait()
        return carry

    lax.fori_loop(1, n, gather_wait, 0)
    centers = cen_all[...].reshape(width, 128).T
    picks = (0, 1, 2, 11)
    coupling = matern([own_cols[:, c : c + 1] for c in picks], [centers[c : c + 1, :] for c in picks])
    global_ids = lax.broadcasted_iota(jnp.int32, (ob, width), 1)
    near = jnp.zeros((ob, width), F32)
    for t in range(ids.shape[1]):
        near = jnp.where(ids[:, t : t + 1] == global_ids, 1.0, near)
    coupling = jnp.where(near > 0.0, 0.0, coupling).astype(BF16)

    step_w = 128
    total = jnp.zeros((ob * half, 2 * np_), F32)
    pick_r = lax.broadcasted_iota(jnp.int32, (step_w, step_w * half), 0)
    pick_c = lax.broadcasted_iota(jnp.int32, (step_w, step_w * half), 1)
    spread = jnp.where(pick_c // half == pick_r, 1.0, 0.0).astype(BF16)
    eye_r = lax.broadcasted_iota(jnp.int32, (ob * half, step_w * half), 0)
    eye_c = lax.broadcasted_iota(jnp.int32, (ob * half, step_w * half), 1)
    same = lax.rem(eye_r, half) == lax.rem(eye_c, half)
    per = step_w // ob
    for q in range(width // step_w):
        wide = nn(coupling[:, q * step_w : (q + 1) * step_w], spread)
        wide = jnp.concatenate(
            [jnp.broadcast_to(wide[i : i + 1, :], (half, step_w * half)) for i in range(ob)], axis=0
        )
        kron = jnp.where(same, wide, 0.0).astype(BF16)
        folded = fold_all[q * per : (q + 1) * per].reshape(step_w * half, 2 * np_)
        total = total + nn(kron, folded)
    summed = total.astype(BF16)

    loads[5].wait()
    for b in range(ob):
        part_copy(b).wait()
    for b in range(ob):
        mine = summed[b * half : (b + 1) * half, :]
        far = tn(mine[:, :np_], bout_ref[b, 0:half, :]) + tn(mine[:, np_:], bout_ref[b, half:, :])
        out_ref[:, b * bs : (b + 1) * bs] = acc[b] + part[b] + far


def solution(mesh):
    n = mesh.shape["row"]

    def shards(coordinates, length_scale, probes, near_ids, near_count, basis_out, basis_in):
        ob, rank, bs = basis_out.shape
        np_ = probes.shape[0]
        own = ob * bs
        slots = near_ids.shape[1]
        vmem = pl.BlockSpec(memory_space=pltpu.VMEM)
        dma = pltpu.SemaphoreType.DMA
        return pl.pallas_call(
            functools.partial(kernel, n, ob, bs),
            out_shape=jax.ShapeDtypeStruct((np_, own), F32),
            in_specs=[pl.BlockSpec(memory_space=pl.ANY)] * 6,
            out_specs=vmem,
            scratch_shapes=[
                pltpu.VMEM((3, own), F32),
                pltpu.VMEM((1, own), F32),
                pltpu.VMEM((np_, own), BF16),
                pltpu.VMEM((ob, slots), jnp.int32),
                pltpu.VMEM((ob, rank, bs), BF16),
                pltpu.VMEM((ob, rank, bs), BF16),
                pltpu.VMEM((3, own), F32),
                pltpu.VMEM((1, own), F32),
                pltpu.VMEM((np_, own), BF16),
                pltpu.VMEM((ob, slots), jnp.int32),
                pltpu.VMEM((ROWS, own), F32),
                pltpu.VMEM((ROWS, 2 * own), F32),
                pltpu.VMEM((ob, ROWS, bs), F32),
                pltpu.VMEM((ob, ROWS, bs), F32),
                pltpu.VMEM((ob, bs, 8 * ROWS), BF16),
                pltpu.VMEM((2 * ob, 8 * ROWS, bs), BF16),
                pltpu.VMEM(((HALO + 1) * ob, 1, bs), F32),
                pltpu.VMEM(((HALO + 1) * 2 * ob, 1, bs), F32),
                pltpu.VMEM((2 * ob, np_, bs), F32),
                pltpu.VMEM((ob, np_, bs), F32),
                pltpu.VMEM((n, ob * rank // 2, 2 * np_), BF16),
                pltpu.VMEM((n, ob, 128), F32),
                pltpu.VMEM((2, bs, bs), BF16),
                dma((6,)), dma((4,)), dma((4,)), dma((ob,)), dma((ob,)),
                dma((n,)), dma((n,)), dma((n,)), dma((n,)),
            ],
            compiler_params=pltpu.CompilerParams(collective_id=0, has_side_effects=True, vmem_limit_bytes=60 * 1024 * 1024),
        )(coordinates, length_scale.reshape(1, own), probes, near_ids, basis_out, basis_in)

    placed = (
        P(None, ("grp", "row")),
        P(("grp", "row")),
        P(None, ("grp", "row")),
        P(("grp", "row"), None),
        P(("grp", "row")),
        P(("grp", "row"), None, None),
        P(("grp", "row"), None, None),
    )
    return jax.shard_map(
        shards, mesh=mesh, in_specs=placed, out_specs=P(None, ("grp", "row")), check_vma=False
    )
```
